256 devices in a mesh: au: 32 (over y, x, core), ia: 8 (over z).
Axes of the slice: x: 4, y: 4, z: 8, core: 2. Of those that a mesh axis runs over, the one named last changes fastest.
Arguments:
- user_emb: float32 [131072, 128], P(('au', 'ia')), may hold values from -6 to 6
- item_emb: float32 [32768, 128], P(('ia', 'au')), may hold values from -6 to 6
- user_degree: int32 [131072], P(('au', 'ia')), may hold values from 1 to 64
- item_degree: int32 [32768], P(('ia', 'au')), may hold values from 1 to 64
- tiles: float32 [32768, 128, 128], P(('au', 'ia')), as said below
- tile_user_block: int32 [32768], P(('au', 'ia')), may hold values from 0 to 31
- tile_item_block: int32 [32768], P(('au', 'ia')), may hold values from 0 to 31
- live_tiles: int32 [256], P(('au', 'ia')), may hold values from 32 to 128, as said below
Outputs:
- user_final: float32 [131072, 128], P(('au', 'ia'))
- item_final: float32 [32768, 128], P(('ia', 'au'))
The draws below stay inside these ranges and needn't reach their ends.
Inputs may be any that keep to these rules, and one draw needn't show every extreme that they name: Tile slots of grid cell c beyond the first live_tiles[c] are unused; some cell uses all 128. `tiles`: each tile holds weights of 0 or between 0.05 and 0.35.
All inputs are finite; a program needn't handle non-finite values.
Results may differ from the reference program's by a relative error of at most 0.0001.
Values sent between devices are 32-bit elements; how exact they have to be, the bound alone decides.
A program may use at most 128 MiB of HBM per device.

```python
import math
import jax
import jax.numpy as jnp
import numpy as np
from jax import lax

D = 128
TILE = 128
LAYERS = 2
NT_DEV = 128
USERS = 131072
ITEMS = 32768
UB = 32
IB = 32
N_AU = 32
N_IA = 8


def draw_tiles(key, part):
    first_key, second_key = jax.random.split(key)
    shape_all = (N_AU * N_IA * NT_DEV, TILE, TILE)
    keep_mask = jax.random.uniform(first_key, shape_all) < 0.5
    values = jax.random.uniform(second_key, shape_all, minval=0.1, maxval=0.3)
    return jnp.where(keep_mask, values, 0.0).astype(jnp.float32)


def draw_live_tiles(key, part):
    first_key, second_key = jax.random.split(jax.random.fold_in(key, 17))
    counts = jax.random.randint(first_key, (N_AU * N_IA,), NT_DEV // 4, NT_DEV + 1, dtype=jnp.int32)
    chosen = jax.random.randint(second_key, (), 0, N_AU * N_IA, dtype=jnp.int32)
    return counts.at[chosen].set(NT_DEV)


def with_ends(entries, key, least, high):
    shape = entries.shape
    spot = [jax.random.randint(jax.random.fold_in(key, axis), (), 0, shape[axis]) for axis in range(len(shape))]
    entries = entries.at[tuple(spot)].set(least)
    longest = shape.index(max(shape))
    spot[longest] = (spot[longest] + 1) % shape[longest]
    return entries.at[tuple(spot)].set(high)


def shard_levels(rng, dims, pieces, smallest, top_value):
    factor_of = 1.0
    for axis_at, blocks in pieces:
        steps = jax.random.uniform(jax.random.fold_in(jax.random.fold_in(rng, 6), axis_at), (blocks,), jnp.float32, smallest / len(pieces), top_value / len(pieces))
        factor_of = factor_of * jnp.repeat(jnp.exp(steps), dims[axis_at] // blocks).reshape((-1,) + (1,) * (len(dims) - 1 - axis_at))
    return factor_of


def rank_bounds(count, skew):
    loads = [(1 << 20) // math.isqrt(standing ** skew) + 1 for standing in range(1, count + 1)]
    scale = 1 + sum(loads) // (1 << 30)
    return np.cumsum(np.array([max(1, weight // scale) for weight in loads]))


def ranked_ids(stream_key, extent, number_of, skew):
    table = rank_bounds(number_of, skew)
    ticket = jax.random.randint(jax.random.fold_in(stream_key, 1), extent, 0, int(table[number_of - 1]))
    grade = jnp.searchsorted(jnp.asarray(table, jnp.int32), ticket, side="right")
    return jax.random.permutation(jax.random.fold_in(stream_key, 2), number_of)[grade].astype(jnp.int32)


def gaussian(key, extent, deviation, bound, shards=(), kind=jnp.bfloat16):
    array = jax.random.normal(key, extent, jnp.float32) * deviation
    if len(shards) > 0:
        array = shard_levels(key, extent, shards, -0.22, 0.18) * array
    return jnp.clip(array, min=-bound, max=bound).astype(kind)


def setup_inputs(seed: int = 0) -> dict:
    keys = jax.random.split(jax.random.key(seed), 9)
    user_emb = gaussian(keys[0], (USERS, D), 1.0, 6.0, ((0, 256),), jnp.float32)
    item_emb = gaussian(keys[1], (ITEMS, D), 1.0, 6.0, ((0, 256),), jnp.float32)
    user_degree = with_ends(jax.random.randint(keys[2], (USERS,), 1, 65), jax.random.fold_in(keys[2], 1), 1, 64).astype(jnp.int32)
    item_degree = with_ends(jax.random.randint(keys[3], (ITEMS,), 1, 65), jax.random.fold_in(keys[3], 1), 1, 64).astype(jnp.int32)
    tiles = draw_tiles(jax.random.fold_in(keys[8], 71), 0)
    tile_user_block = with_ends(ranked_ids(keys[5], (N_AU * N_IA * NT_DEV,), UB, 2), jax.random.fold_in(keys[5], 3), 0, UB - 1).astype(jnp.int32)
    tile_item_block = with_ends(jax.random.randint(keys[6], (N_AU * N_IA * NT_DEV,), 0, IB), jax.random.fold_in(keys[6], 1), 0, IB - 1).astype(jnp.int32)
    live_tiles = draw_live_tiles(jax.random.fold_in(keys[8], 71), 0)
    return dict(user_emb=user_emb, item_emb=item_emb, user_degree=user_degree, item_degree=item_degree, tiles=tiles, tile_user_block=tile_user_block, tile_item_block=tile_item_block, live_tiles=live_tiles)


def reference(user_emb, item_emb, user_degree, item_degree, tiles, tile_user_block, tile_item_block, live_tiles):
    cells = N_AU * N_IA
    norm_user = lax.rsqrt(user_degree.astype(jnp.float32))[:, None]
    norm_item = lax.rsqrt(item_degree.astype(jnp.float32))[:, None]
    owner_ids = jnp.arange(cells, dtype=jnp.int32)
    row_base = owner_ids // N_IA * UB
    col_base = owner_ids % N_IA * IB
    user_ids = (tile_user_block.reshape(cells, NT_DEV) + row_base[:, None]).astype(jnp.int32)
    item_ids = (tile_item_block.reshape(cells, NT_DEV) + col_base[:, None]).astype(jnp.int32)
    live_mask = (jnp.arange(NT_DEV, dtype=jnp.int32)[None, :] < live_tiles[:, None]).astype(jnp.float32)
    grouped = tiles.reshape(cells, NT_DEV, TILE, TILE)

    def propagate(users_now, items_now):
        scaled_users = (users_now * norm_user).reshape(-1, TILE, D)
        scaled_items = (items_now * norm_item).reshape(-1, TILE, D)

        def scan_step(running, batch_group):
            user_acc, item_acc = running
            weights, user_rows, item_rows, live_row = batch_group
            weights = weights * live_row[:, None, None]
            to_users = jnp.einsum('tuk,tkd->tud', weights, scaled_items[item_rows], precision=lax.Precision.HIGHEST)
            to_items = jnp.einsum('tuk,tud->tkd', weights, scaled_users[user_rows], precision=lax.Precision.HIGHEST)
            return ((user_acc.at[user_rows].add(to_users), item_acc.at[item_rows].add(to_items)), None)
        start = (jnp.zeros(scaled_users.shape, jnp.float32), jnp.zeros(scaled_items.shape, jnp.float32))
        (user_acc, item_acc), _ = lax.scan(scan_step, start, (grouped, user_ids, item_ids, live_mask))
        return (user_acc.reshape(users_now.shape) * norm_user, item_acc.reshape(items_now.shape) * norm_item)
    users_now, items_now = (user_emb, item_emb)
    user_total, item_total = (user_emb, item_emb)
    for layer_index in range(LAYERS):
        users_now, items_now = propagate(users_now, items_now)
        user_total = user_total + users_now
        item_total = item_total + items_now
    return (user_total / (LAYERS + 1.0), item_total / (LAYERS + 1.0))
```

```python
import functools
import heapq

import jax
import jax.numpy as jnp
from jax import lax
from jax.experimental import pallas as pl
from jax.experimental.pallas import tpu as pltpu
from jax.sharding import PartitionSpec as P

MESH = pl.DeviceIdType.MESH
LAYERS = 2
T = 128
NZ = 8
NX, NY = 4, 4
CHIPS = NX * NY
AU = 2 * CHIPS
UB = 32
IB = 32
SLOTS = 128
PER_Z = UB // NZ
RC = 4
ROWS = PER_Z * T // (2 * RC)
OFFSETS = sorted(
    ((dx, dy) for dx in range(NX) for dy in range(NY)),
    key=lambda o: -(min(o[0], NX - o[0]) + min(o[1], NY - o[1])),
)
PEERS = OFFSETS[:-1]
AG_RIGHT = [(s, c) for s in range(NZ // 2) for c in range(PER_Z) if s < NZ // 2 - 1 or c < PER_Z // 2]
AG_LEFT = [(s, c) for s in range(NZ // 2) for c in range(PER_Z) if s < NZ // 2 - 1 or c >= PER_Z // 2]
PIECE = 16
UNROLL = 4


def halves(value):
    high = value.astype(jnp.bfloat16)
    low = (value - high.astype(jnp.float32)).astype(jnp.bfloat16)
    return jnp.concatenate([high, low], axis=1)


def column(row):
    return jnp.transpose(jnp.broadcast_to(row, (T, T)))


def merge(chains):
    heap = []
    for at, (start, gen) in enumerate(chains):
        heap.append((start, at, gen))
    heapq.heapify(heap)
    while heap:
        when, at, gen = heapq.heappop(heap)
        step = next(gen, None)
        if step is not None:
            heapq.heappush(heap, (when + step, at, gen))


class Place:
    def __init__(self):
        self.au = lax.axis_index("au")
        self.z = lax.axis_index("ia")
        self.core = lax.rem(self.au, 2)
        self.x = lax.rem(self.au // 2, NX)
        self.y = self.au // (2 * NX)
        self.partner = self.au + 1 - 2 * self.core

    def chip(self, dx, dy):
        return lax.rem(self.y + dy, NY) * NX + lax.rem(self.x + dx, NX)

    def ring(self, step):
        return lax.rem(self.z + NZ + step, NZ)


class GatherZ:
    def __init__(self, me, buf, sems, on_chunk):
        self.me, self.buf, self.sems, self.on_chunk = me, buf, sems, on_chunk
        self.plans = (AG_RIGHT, AG_LEFT)

    def copy(self, way, k, received=False):
        me = self.me
        s, c = self.plans[way][k]
        sign = 1 if way == 0 else -1
        block = me.ring(-sign * (s + (1 if received else 0)))
        ref = self.buf.at[block, pl.ds(c * T, T)]
        return (
            pltpu.make_async_remote_copy(
                src_ref=ref,
                dst_ref=ref,
                send_sem=self.sems.at[2 * way, k],
                recv_sem=self.sems.at[2 * way + 1, k],
                device_id=(me.au, me.ring(sign)),
                device_id_type=MESH,
            ),
            block,
            c,
        )

    def start_own(self, c):
        for way in range(2):
            self.copy(way, self.plans[way].index((0, c)))[0].start()

    def run(self, dt):
        order = []
        for k in range(len(AG_RIGHT)):
            order += [(0, k), (1, k)]
        for way, k in order:
            yield dt / 2
            s, c = self.plans[way][k]
            copy, block, c = self.copy(way, k, received=True)
            copy.wait_recv()
            if (s + 1, c) in self.plans[way]:
                self.copy(way, self.plans[way].index((s + 1, c)))[0].start()
            self.on_chunk(block, c)

    def finish(self):
        for way in range(2):
            for k in range(len(self.plans[way])):
                self.copy(way, k)[0].wait_send()


class ScatterZ:
    def __init__(self, me, q, land, sems, on_final):
        self.me, self.q, self.land, self.sems, self.on_final = me, q, land, sems, on_final

    def part(self, block, way, c):
        rows = way * RC * ROWS + c * ROWS
        return self.q.at[block * PER_Z + rows // T, pl.ds(rows % T, ROWS)]

    def copy(self, way, s, c):
        me = self.me
        sign = 1 if way == 0 else -1
        if s == 0:
            src = self.part(me.ring(-sign), way, c)
        else:
            src = self.land.at[way, s - 1, c]
        return pltpu.make_async_remote_copy(
            src_ref=src,
            dst_ref=self.land.at[way, s, c],
            send_sem=self.sems.at[2 * way, s * RC + c],
            recv_sem=self.sems.at[2 * way + 1, s * RC + c],
            device_id=(me.au, me.ring(sign)),
            device_id_type=MESH,
        )

    def start(self):
        for c in range(RC):
            for way in range(2):
                self.copy(way, 0, c).start()

    def run(self, dt):
        me = self.me
        for s in range(NZ - 1):
            for c in range(RC):
                for way in range(2):
                    yield dt / 2
                    sign = 1 if way == 0 else -1
                    self.copy(way, s, c).wait_recv()
                    mine = self.part(me.ring(-sign * (s + 2)), way, c)
                    value = self.land[way, s, c] + mine[...]
                    if s < NZ - 2:
                        self.land[way, s, c] = value
                        self.copy(way, s + 1, c).start()
                    else:
                        self.on_final(way * RC * ROWS + c * ROWS, value)

    def finish(self):
        for s in range(NZ - 1):
            for c in range(RC):
                for way in range(2):
                    self.copy(way, s, c).wait_send()


class GatherPlane:
    def __init__(self, me, buf, sems, on_block):
        self.me, self.buf, self.sems, self.on_block = me, buf, sems, on_block

    def send(self, k):
        me = self.me
        dx, dy = PEERS[k]
        ref = self.buf.at[me.au]
        return pltpu.make_async_remote_copy(
            src_ref=ref, dst_ref=ref,
            send_sem=self.sems.at[0, k], recv_sem=self.sems.at[1, k],
            device_id=(2 * me.chip(dx, dy) + me.core, me.z), device_id_type=MESH,
        )

    def source(self, k):
        dx, dy = OFFSETS[k]
        return 2 * self.me.chip(NX - dx, NY - dy)

    def landed(self, k):
        me = self.me
        dx, dy = PEERS[k]
        ref = self.buf.at[self.source(k) + me.core]
        return pltpu.make_async_remote_copy(
            src_ref=ref, dst_ref=ref,
            send_sem=self.sems.at[0, k], recv_sem=self.sems.at[1, k],
            device_id=(2 * me.chip(dx, dy) + me.core, me.z), device_id_type=MESH,
        )

    def across(self, k, received=False):
        me = self.me
        side = 1 - me.core if received else me.core
        ref = self.buf.at[self.source(k) + side]
        return pltpu.make_async_remote_copy(
            src_ref=ref, dst_ref=ref,
            send_sem=self.sems.at[2, k], recv_sem=self.sems.at[3, k],
            device_id=(me.partner, me.z), device_id_type=MESH,
        )

    def start(self):
        for k in range(len(PEERS)):
            self.send(k).start()
        self.across(CHIPS - 1).start()

    def run(self, dt, dt_across):
        me = self.me
        self.on_block(me.au)
        for k in reversed(range(len(PEERS))):
            yield dt
            self.landed(k).wait_recv()
            self.across(k).start()
            self.on_block(self.source(k) + me.core)
        for k in reversed(range(CHIPS)):
            yield dt_across
            self.across(k, received=True).wait_recv()
            self.on_block(self.source(k) + 1 - me.core)

    def finish(self):
        for k in range(len(PEERS)):
            self.send(k).wait_send()
        for k in range(CHIPS):
            self.across(k).wait_send()


class ScatterPlane:
    def __init__(self, me, p, pair, home, sems, on_final):
        self.me, self.p, self.pair, self.home = me, p, pair, home
        self.sems, self.on_final = sems, on_final

    def across(self, k):
        me = self.me
        dx, dy = OFFSETS[k]
        return pltpu.make_async_remote_copy(
            src_ref=self.p.at[2 * me.chip(dx, dy) + 1 - me.core], dst_ref=self.pair.at[k],
            send_sem=self.sems.at[0, k], recv_sem=self.sems.at[1, k],
            device_id=(me.partner, me.z), device_id_type=MESH,
        )

    def send(self, k):
        me = self.me
        dx, dy = PEERS[k]
        return pltpu.make_async_remote_copy(
            src_ref=self.pair.at[k], dst_ref=self.home.at[k],
            send_sem=self.sems.at[2, k], recv_sem=self.sems.at[3, k],
            device_id=(2 * me.chip(dx, dy) + me.core, me.z), device_id_type=MESH,
        )

    def start(self):
        for k in range(CHIPS):
            self.across(k).start()

    def run(self, dt_across, dt):
        me = self.me
        for k in range(CHIPS):
            yield dt_across
            self.across(k).wait_recv()
            dx, dy = OFFSETS[k]
            self.pair[k] = self.pair[k] + self.p[2 * me.chip(dx, dy) + me.core]
            if k < len(PEERS):
                self.send(k).start()
        for k in reversed(range(len(PEERS))):
            yield dt
            self.send(k).wait_recv()
            self.pair[CHIPS - 1] = self.pair[CHIPS - 1] + self.home[k]
        self.on_final(self.pair[CHIPS - 1])

    def finish(self):
        for k in range(CHIPS):
            self.across(k).wait_send()
        for k in range(len(PEERS)):
            self.send(k).wait_send()


def kernel(
    table, user_emb, item_emb, user_degree, item_degree, tiles_hbm,
    user_out, item_out,
    tiles, run, ug, vg, u2, v2, q, p, land, pair, home, user_scale, item_scale,
    tile_sem, gz_sems, sz_sems, gp_sems, sp_sems,
):
    me = Place()
    load = pltpu.make_async_copy(tiles_hbm, tiles, tile_sem)
    load.start()

    barrier = pltpu.get_barrier_semaphore()
    greeted = [(me.au, me.ring(1)), (me.au, me.ring(-1)), (me.partner, me.z)]
    greeted += [(2 * me.chip(dx, dy) + me.core, me.z) for dx, dy in PEERS]
    for device in greeted:
        pl.semaphore_signal(barrier, inc=1, device_id=device, device_id_type=MESH)

    item_scale[...] = column(lax.rsqrt(item_degree[...].astype(jnp.float32)))
    vg[0, me.au] = item_emb[...] * item_scale[...]
    for c in range(PER_Z):
        rows = pl.ds(c * T, T)
        user_scale[rows] = column(lax.rsqrt(user_degree[c : c + 1].astype(jnp.float32)))
        ug[0, me.z, rows] = user_emb[rows] * user_scale[rows]
    user_out[...] = user_emb[...]
    item_out[...] = item_emb[...]
    run[0] = jnp.zeros((T, T), jnp.float32)
    pl.semaphore_wait(barrier, len(greeted))

    def user_chunk(layer):
        def take(block, c):
            u2[block * PER_Z + c] = halves(ug[layer, block, pl.ds(c * T, T)])
        return take

    def item_block(layer):
        def take(block):
            v2[block] = halves(vg[layer, block])
        return take

    gather_z = [GatherZ(me, ug.at[l], gz_sems.at[l], user_chunk(l)) for l in range(LAYERS)]
    gather_plane = [GatherPlane(me, vg.at[l], gp_sems.at[l], item_block(l)) for l in range(LAYERS)]

    def user_final(layer):
        last = layer + 1 == LAYERS
        def take(row, value):
            rows = pl.ds(row, ROWS)
            scale = user_scale[rows]
            now = value * scale
            total = user_out[rows] + now
            user_out[rows] = total * (1.0 / (LAYERS + 1.0)) if last else total
            if not last:
                ug[layer + 1, me.z, rows] = now * scale
                if (row + ROWS) % T == 0:
                    gather_z[layer + 1].start_own(row // T)
                    user_chunk(layer + 1)(me.z, row // T)
        return take

    def item_final(layer):
        last = layer + 1 == LAYERS
        def take(value):
            now = value * item_scale[...]
            total = item_out[...] + now
            item_out[...] = total * (1.0 / (LAYERS + 1.0)) if last else total
            if not last:
                vg[layer + 1, me.au] = now * item_scale[...]
                gather_plane[layer + 1].start()
        return take

    scatter_z = [ScatterZ(me, q.at[l], land.at[l], sz_sems.at[l], user_final(l)) for l in range(LAYERS)]
    scatter_plane = [
        ScatterPlane(me, p.at[l], pair.at[l], home.at[l], sp_sems.at[l], item_final(l)) for l in range(LAYERS)
    ]

    def products(kind, source, out, dt):
        base = 4 * kind
        def step(at, carry):
            acc = run[at * UNROLL]
            for i in range(UNROLL):
                slot = at * UNROLL + i
                w = tiles[table[base, slot]]
                if kind == 1:
                    w = jnp.transpose(w)
                rows = source[table[base + 1, slot]]
                wide = jnp.dot(
                    halves(w), jnp.concatenate([rows, rows], axis=0), preferred_element_type=jnp.float32
                )
                keep = table[base + 2, slot].astype(jnp.float32)
                acc = acc * keep + (wide[:, :T] + wide[:, T:])
                run[slot + 1] = acc
            return carry
        per = PIECE // UNROLL
        for piece in range(SLOTS // PIECE):
            yield dt
            lax.fori_loop(piece * per, (piece + 1) * per, step, 0)
        def pick(block, carry):
            out[block] = run[table[base + 3, block]]
            return carry
        yield dt
        lax.fori_loop(0, UB, pick, 0)

    for c in range(PER_Z):
        gather_z[0].start_own(c)
        user_chunk(0)(me.z, c)
    gather_plane[0].start()

    def items_then_products(layer, first):
        yield 1e-3
        yield from first
        yield from gather_plane[layer].run(0.9, 0.1)
        if layer == 0:
            load.wait()
        yield from products(0, v2, q.at[layer], 0.35)
        scatter_z[layer].start()

    def empty():
        return
        yield

    merge([(0.0, items_then_products(0, empty())), (1.0, gather_z[0].run(1.4))])

    def plane_chain():
        yield from products(1, u2, p.at[0], 0.35)
        scatter_plane[0].start()
        yield from items_then_products(1, scatter_plane[0].run(0.3, 0.7))

    def z_chain():
        yield from scatter_z[0].run(0.7)
        yield from gather_z[1].run(1.4)

    merge([(0.0, plane_chain()), (1.0, z_chain())])

    def last_plane():
        yield from products(1, u2, p.at[1], 0.35)
        scatter_plane[1].start()
        yield from scatter_plane[1].run(0.3, 0.7)

    merge([(0.0, last_plane()), (1.0, scatter_z[1].run(0.7))])

    for layer in range(LAYERS):
        for chain in (gather_z, gather_plane, scatter_z, scatter_plane):
            chain[layer].finish()


def sorted_slots(keys, others):
    slots = jnp.arange(SLOTS, dtype=jnp.int32)
    before = (keys[:, None] < keys[None, :]) | (
        (keys[:, None] == keys[None, :]) & (slots[:, None] < slots[None, :])
    )
    place = jnp.sum(before.astype(jnp.int32), axis=0)
    hit = (place[:, None] == slots[None, :]).astype(jnp.int32)
    order = jnp.sum(hit * slots[:, None], axis=0)
    block = jnp.sum(hit * others[:, None], axis=0)
    key_sorted = jnp.sum(hit * keys[:, None], axis=0)
    first = jnp.sum((keys[:, None] < key_sorted[None, :]).astype(jnp.int32), axis=0) == slots
    upto = jnp.sum((keys[:, None] <= slots[None, :]).astype(jnp.int32), axis=0)
    any_of = jnp.sum((keys[:, None] == slots[None, :]).astype(jnp.int32), axis=0) > 0
    return [order, block, 1 - first.astype(jnp.int32), jnp.where(any_of, upto, 0)]


def per_device(
    user_emb, item_emb, user_degree, item_degree, tiles, tile_user_block, tile_item_block, live_tiles
):
    live = jnp.arange(SLOTS, dtype=jnp.int32) < live_tiles[0]
    by_user = sorted_slots(jnp.where(live, tile_user_block, UB), tile_item_block)
    by_item = sorted_slots(jnp.where(live, tile_item_block, IB), tile_user_block)
    table = jnp.stack(by_user + by_item)
    f32 = jnp.float32
    vmem = pl.BlockSpec(memory_space=pltpu.VMEM)
    dma = pltpu.SemaphoreType.DMA
    return pl.pallas_call(
        kernel,
        out_shape=[
            jax.ShapeDtypeStruct((PER_Z * T, T), f32),
            jax.ShapeDtypeStruct((T, T), f32),
        ],
        in_specs=[pl.BlockSpec(memory_space=pltpu.SMEM)] + [vmem] * 4 + [pl.BlockSpec(memory_space=pl.ANY)],
        out_specs=[vmem, vmem],
        scratch_shapes=[
            pltpu.VMEM((SLOTS, T, T), f32),
            pltpu.VMEM((SLOTS + 1, T, T), f32),
            pltpu.VMEM((LAYERS, NZ, PER_Z * T, T), f32),
            pltpu.VMEM((LAYERS, AU, T, T), f32),
            pltpu.VMEM((UB, T, 2 * T), jnp.bfloat16),
            pltpu.VMEM((IB, T, 2 * T), jnp.bfloat16),
            pltpu.VMEM((LAYERS, UB, T, T), f32),
            pltpu.VMEM((LAYERS, IB, T, T), f32),
            pltpu.VMEM((LAYERS, 2, NZ - 1, RC, ROWS, T), f32),
            pltpu.VMEM((LAYERS, CHIPS, T, T), f32),
            pltpu.VMEM((LAYERS, CHIPS - 1, T, T), f32),
            pltpu.VMEM((PER_Z * T, T), f32),
            pltpu.VMEM((T, T), f32),
            dma,
            dma((LAYERS, 4, len(AG_RIGHT))),
            dma((LAYERS, 4, (NZ - 1) * RC)),
            dma((LAYERS, 4, CHIPS)),
            dma((LAYERS, 4, CHIPS)),
        ],
        compiler_params=pltpu.CompilerParams(
            collective_id=0, has_side_effects=True, vmem_limit_bytes=62 << 20
        ),
    )(
        table, user_emb, item_emb, user_degree.reshape(PER_Z, T), item_degree.reshape(1, T), tiles
    )


def solution(mesh):
    in_specs = (
        P(("au", "ia"), None),
        P(("ia", "au"), None),
        P(("au", "ia")),
        P(("ia", "au")),
        P(("au", "ia"), None, None),
        P(("au", "ia")),
        P(("au", "ia")),
        P(("au", "ia")),
    )
    out_specs = (P(("au", "ia"), None), P(("ia", "au"), None))
    return jax.shard_map(
        per_device, mesh=mesh, in_specs=in_specs, out_specs=out_specs, check_vma=False
    )
```

```python
import functools
import heapq

import jax
import jax.numpy as jnp
from jax import lax
from jax.experimental import pallas as pl
from jax.experimental.pallas import tpu as pltpu
from jax.sharding import PartitionSpec as P

MESH = pl.DeviceIdType.MESH
LAYERS = 2
T = 128
NZ = 8
NX, NY = 4, 4
CHIPS = NX * NY
AU = 2 * CHIPS
UB = 32
IB = 32
SLOTS = 128
PER_Z = UB // NZ
RC = 4
ROWS = PER_Z * T // (2 * RC)
OFFSETS = sorted(
    ((dx, dy) for dx in range(NX) for dy in range(NY)),
    key=lambda o: -(min(o[0], NX - o[0]) + min(o[1], NY - o[1])),
)
PEERS = OFFSETS[:-1]
AG_RIGHT = [(s, c) for s in range(NZ // 2) for c in range(PER_Z) if s < NZ // 2 - 1 or c < PER_Z // 2]
AG_LEFT = [(s, c) for s in range(NZ // 2) for c in range(PER_Z) if s < NZ // 2 - 1 or c >= PER_Z // 2]
PIECE = 32
UNROLL = 32


def halves(value):
    high = value.astype(jnp.bfloat16)
    low = (value - high.astype(jnp.float32)).astype(jnp.bfloat16)
    return jnp.concatenate([high, low], axis=1)


def column(row):
    return jnp.transpose(jnp.broadcast_to(row, (T, T)))


def merge(chains):
    heap = []
    for at, (start, gen) in enumerate(chains):
        heap.append((start, at, gen))
    heapq.heapify(heap)
    while heap:
        when, at, gen = heapq.heappop(heap)
        step = next(gen, None)
        if step is not None:
            heapq.heappush(heap, (when + step, at, gen))


class Place:
    def __init__(self):
        self.au = lax.axis_index("au")
        self.z = lax.axis_index("ia")
        self.core = lax.rem(self.au, 2)
        self.x = lax.rem(self.au // 2, NX)
        self.y = self.au // (2 * NX)
        self.partner = self.au + 1 - 2 * self.core

    def chip(self, dx, dy):
        return lax.rem(self.y + dy, NY) * NX + lax.rem(self.x + dx, NX)

    def ring(self, step):
        return lax.rem(self.z + NZ + step, NZ)


class GatherZ:
    def __init__(self, me, buf, sems, on_chunk):
        self.me, self.buf, self.sems, self.on_chunk = me, buf, sems, on_chunk
        self.plans = (AG_RIGHT, AG_LEFT)

    def copy(self, way, k, received=False):
        me = self.me
        s, c = self.plans[way][k]
        sign = 1 if way == 0 else -1
        block = me.ring(-sign * (s + (1 if received else 0)))
        ref = self.buf.at[block, pl.ds(c * T, T)]
        return (
            pltpu.make_async_remote_copy(
                src_ref=ref,
                dst_ref=ref,
                send_sem=self.sems.at[2 * way, k],
                recv_sem=self.sems.at[2 * way + 1, k],
                device_id=(me.au, me.ring(sign)),
                device_id_type=MESH,
            ),
            block,
            c,
        )

    def start_own(self, c):
        for way in range(2):
            self.copy(way, self.plans[way].index((0, c)))[0].start()

    def run(self, dt):
        order = []
        for k in range(len(AG_RIGHT)):
            order += [(0, k), (1, k)]
        for way, k in order:
            yield dt / 2
            s, c = self.plans[way][k]
            copy, block, c = self.copy(way, k, received=True)
            copy.wait_recv()
            if (s + 1, c) in self.plans[way]:
                self.copy(way, self.plans[way].index((s + 1, c)))[0].start()
            self.on_chunk(block, c)

    def finish(self):
        for way in range(2):
            for k in range(len(self.plans[way])):
                self.copy(way, k)[0].wait_send()


class ScatterZ:
    def __init__(self, me, q, land, sems, on_final):
        self.me, self.q, self.land, self.sems, self.on_final = me, q, land, sems, on_final

    def part(self, block, way, c):
        rows = way * RC * ROWS + c * ROWS
        return self.q.at[block * PER_Z + rows // T, pl.ds(rows % T, ROWS)]

    def copy(self, way, s, c):
        me = self.me
        sign = 1 if way == 0 else -1
        if s == 0:
            src = self.part(me.ring(-sign), way, c)
        else:
            src = self.land.at[way, s - 1, c]
        return pltpu.make_async_remote_copy(
            src_ref=src,
            dst_ref=self.land.at[way, s, c],
            send_sem=self.sems.at[2 * way, s * RC + c],
            recv_sem=self.sems.at[2 * way + 1, s * RC + c],
            device_id=(me.au, me.ring(sign)),
            device_id_type=MESH,
        )

    def start(self):
        for c in range(RC):
            for way in range(2):
                self.copy(way, 0, c).start()

    def run(self, dt):
        me = self.me
        for s in range(NZ - 1):
            for c in range(RC):
                for way in range(2):
                    yield dt / 2
                    sign = 1 if way == 0 else -1
                    self.copy(way, s, c).wait_recv()
                    mine = self.part(me.ring(-sign * (s + 2)), way, c)
                    value = self.land[way, s, c] + mine[...]
                    if s < NZ - 2:
                        self.land[way, s, c] = value
                        self.copy(way, s + 1, c).start()
                    else:
                        self.on_final(way * RC * ROWS + c * ROWS, value)

    def finish(self):
        for s in range(NZ - 1):
            for c in range(RC):
                for way in range(2):
                    self.copy(way, s, c).wait_send()


class GatherPlane:
    def __init__(self, me, buf, sems, on_block):
        self.me, self.buf, self.sems, self.on_block = me, buf, sems, on_block

    def send(self, k):
        me = self.me
        dx, dy = PEERS[k]
        ref = self.buf.at[me.au]
        return pltpu.make_async_remote_copy(
            src_ref=ref, dst_ref=ref,
            send_sem=self.sems.at[0, k], recv_sem=self.sems.at[1, k],
            device_id=(2 * me.chip(dx, dy) + me.core, me.z), device_id_type=MESH,
        )

    def source(self, k):
        dx, dy = OFFSETS[k]
        return 2 * self.me.chip(NX - dx, NY - dy)

    def landed(self, k):
        me = self.me
        dx, dy = PEERS[k]
        ref = self.buf.at[self.source(k) + me.core]
        return pltpu.make_async_remote_copy(
            src_ref=ref, dst_ref=ref,
            send_sem=self.sems.at[0, k], recv_sem=self.sems.at[1, k],
            device_id=(2 * me.chip(dx, dy) + me.core, me.z), device_id_type=MESH,
        )

    def across(self, k, received=False):
        me = self.me
        side = 1 - me.core if received else me.core
        ref = self.buf.at[self.source(k) + side]
        return pltpu.make_async_remote_copy(
            src_ref=ref, dst_ref=ref,
            send_sem=self.sems.at[2, k], recv_sem=self.sems.at[3, k],
            device_id=(me.partner, me.z), device_id_type=MESH,
        )

    def start(self):
        for k in range(len(PEERS)):
            self.send(k).start()
        self.across(CHIPS - 1).start()

    def run(self, dt, dt_across):
        me = self.me
        self.on_block(me.au)
        yield 2.0
        for k in range(len(PEERS)):
            yield dt
            self.landed(k).wait_recv()
            self.across(k).start()
            self.on_block(self.source(k) + me.core)
        for k in [CHIPS - 1] + list(range(len(PEERS))):
            yield dt_across
            self.across(k, received=True).wait_recv()
            self.on_block(self.source(k) + 1 - me.core)

    def finish(self):
        for k in range(len(PEERS)):
            self.send(k).wait_send()
        for k in range(CHIPS):
            self.across(k).wait_send()


class ScatterPlane:
    def __init__(self, me, p, pair, home, sems, on_final):
        self.me, self.p, self.pair, self.home = me, p, pair, home
        self.sems, self.on_final = sems, on_final

    def across(self, k):
        me = self.me
        dx, dy = OFFSETS[k]
        return pltpu.make_async_remote_copy(
            src_ref=self.p.at[2 * me.chip(dx, dy) + 1 - me.core], dst_ref=self.pair.at[k],
            send_sem=self.sems.at[0, k], recv_sem=self.sems.at[1, k],
            device_id=(me.partner, me.z), device_id_type=MESH,
        )

    def send(self, k):
        me = self.me
        dx, dy = PEERS[k]
        return pltpu.make_async_remote_copy(
            src_ref=self.pair.at[k], dst_ref=self.home.at[k],
            send_sem=self.sems.at[2, k], recv_sem=self.sems.at[3, k],
            device_id=(2 * me.chip(dx, dy) + me.core, me.z), device_id_type=MESH,
        )

    def start(self):
        for k in range(CHIPS):
            self.across(k).start()

    def run(self, dt_across, dt):
        me = self.me
        for k in range(CHIPS):
            yield dt_across
            self.across(k).wait_recv()
            dx, dy = OFFSETS[k]
            self.pair[k] = self.pair[k] + self.p[2 * me.chip(dx, dy) + me.core]
            if k < len(PEERS):
                self.send(k).start()
        for k in range(len(PEERS)):
            yield dt
            self.send(k).wait_recv()
            self.pair[CHIPS - 1] = self.pair[CHIPS - 1] + self.home[k]
        self.on_final(self.pair[CHIPS - 1])

    def finish(self):
        for k in range(CHIPS):
            self.across(k).wait_send()
        for k in range(len(PEERS)):
            self.send(k).wait_send()


def kernel(
    table, user_emb, item_emb, user_degree, item_degree, tiles_hbm,
    user_out, item_out,
    tiles, run, ug, vg, u2, v2, q, p, land, pair, home, user_scale, item_scale,
    tile_sem, gz_sems, sz_sems, gp_sems, sp_sems,
):
    me = Place()
    load = pltpu.make_async_copy(tiles_hbm, tiles, tile_sem)
    load.start()

    barrier = pltpu.get_barrier_semaphore()
    greeted = [(me.au, me.ring(1)), (me.au, me.ring(-1)), (me.partner, me.z)]
    greeted += [(2 * me.chip(dx, dy) + me.core, me.z) for dx, dy in PEERS]
    for device in greeted:
        pl.semaphore_signal(barrier, inc=1, device_id=device, device_id_type=MESH)

    item_scale[...] = column(lax.rsqrt(item_degree[...].astype(jnp.float32)))
    vg[0, me.au] = item_emb[...] * item_scale[...]
    for c in range(PER_Z):
        rows = pl.ds(c * T, T)
        user_scale[rows] = column(lax.rsqrt(user_degree[c : c + 1].astype(jnp.float32)))
        ug[0, me.z, rows] = user_emb[rows] * user_scale[rows]
    user_out[...] = user_emb[...]
    item_out[...] = item_emb[...]
    run[0] = jnp.zeros((T, T), jnp.float32)
    pl.semaphore_wait(barrier, len(greeted))

    def user_chunk(layer):
        def take(block, c):
            u2[block * PER_Z + c] = halves(ug[layer, block, pl.ds(c * T, T)])
        return take

    def item_block(layer):
        def take(block):
            v2[block] = halves(vg[layer, block])
        return take

    gather_z = [GatherZ(me, ug.at[l], gz_sems.at[l], user_chunk(l)) for l in range(LAYERS)]
    gather_plane = [GatherPlane(me, vg.at[l], gp_sems.at[l], item_block(l)) for l in range(LAYERS)]

    def user_final(layer):
        last = layer + 1 == LAYERS
        def take(row, value):
            rows = pl.ds(row, ROWS)
            scale = user_scale[rows]
            now = value * scale
            total = user_out[rows] + now
            user_out[rows] = total * (1.0 / (LAYERS + 1.0)) if last else total
            if not last:
                ug[layer + 1, me.z, rows] = now * scale
                if (row + ROWS) % T == 0:
                    gather_z[layer + 1].start_own(row // T)
                    user_chunk(layer + 1)(me.z, row // T)
        return take

    def item_final(layer):
        last = layer + 1 == LAYERS
        def take(value):
            now = value * item_scale[...]
            total = item_out[...] + now
            item_out[...] = total * (1.0 / (LAYERS + 1.0)) if last else total
            if not last:
                vg[layer + 1, me.au] = now * item_scale[...]
                gather_plane[layer + 1].start()
        return take

    scatter_z = [ScatterZ(me, q.at[l], land.at[l], sz_sems.at[l], user_final(l)) for l in range(LAYERS)]
    scatter_plane = [
        ScatterPlane(me, p.at[l], pair.at[l], home.at[l], sp_sems.at[l], item_final(l)) for l in range(LAYERS)
    ]

    def products(kind, source, out, dt):
        base = 4 * kind
        def step(at, carry):
            acc = run[at * UNROLL]
            for i in range(UNROLL):
                slot = at * UNROLL + i
                w = tiles[table[base, slot]]
                if kind == 1:
                    w = jnp.transpose(w)
                rows = source[table[base + 1, slot]]
                wide = jnp.dot(
                    halves(w), jnp.concatenate([rows, rows], axis=0), preferred_element_type=jnp.float32
                )
                keep = table[base + 2, slot].astype(jnp.float32)
                acc = acc * keep + (wide[:, :T] + wide[:, T:])
                run[slot + 1] = acc
            return carry
        per = PIECE // UNROLL
        for piece in range(SLOTS // PIECE):
            yield dt
            lax.fori_loop(piece * per, (piece + 1) * per, step, 0)
        def pick(block, carry):
            out[block] = run[table[base + 3, block]]
            return carry
        yield 0.4
        lax.fori_loop(0, UB, pick, 0)

    for c in range(PER_Z):
        gather_z[0].start_own(c)
        user_chunk(0)(me.z, c)
    gather_plane[0].start()

    def items_then_products(layer, first):
        yield 1e-3
        yield from first
        yield from gather_plane[layer].run(0.9, 0.1)
        if layer == 0:
            load.wait()
        yield from products(0, v2, q.at[layer], 0.9)
        scatter_z[layer].start()

    def empty():
        return
        yield

    merge([(0.0, items_then_products(0, empty())), (1.0, gather_z[0].run(1.6))])

    def plane_chain():
        yield from products(1, u2, p.at[0], 0.9)
        scatter_plane[0].start()
        yield from items_then_products(1, scatter_plane[0].run(0.3, 0.7))

    def z_chain():
        yield from scatter_z[0].run(0.86)
        yield from gather_z[1].run(1.6)

    merge([(0.0, plane_chain()), (1.0, z_chain())])

    def last_plane():
        yield from products(1, u2, p.at[1], 0.9)
        scatter_plane[1].start()
        yield from scatter_plane[1].run(0.3, 0.7)

    merge([(0.0, last_plane()), (1.0, scatter_z[1].run(0.86))])

    for layer in range(LAYERS):
        for chain in (gather_z, gather_plane, scatter_z, scatter_plane):
            chain[layer].finish()


def sorted_slots(keys, others):
    slots = jnp.arange(SLOTS, dtype=jnp.int32)
    before = (keys[:, None] < keys[None, :]) | (
        (keys[:, None] == keys[None, :]) & (slots[:, None] < slots[None, :])
    )
    place = jnp.sum(before.astype(jnp.int32), axis=0)
    hit = (place[:, None] == slots[None, :]).astype(jnp.int32)
    order = jnp.sum(hit * slots[:, None], axis=0)
    block = jnp.sum(hit * others[:, None], axis=0)
    key_sorted = jnp.sum(hit * keys[:, None], axis=0)
    first = jnp.sum((keys[:, None] < key_sorted[None, :]).astype(jnp.int32), axis=0) == slots
    upto = jnp.sum((keys[:, None] <= slots[None, :]).astype(jnp.int32), axis=0)
    any_of = jnp.sum((keys[:, None] == slots[None, :]).astype(jnp.int32), axis=0) > 0
    return [order, block, 1 - first.astype(jnp.int32), jnp.where(any_of, upto, 0)]


def per_device(
    user_emb, item_emb, user_degree, item_degree, tiles, tile_user_block, tile_item_block, live_tiles
):
    live = jnp.arange(SLOTS, dtype=jnp.int32) < live_tiles[0]
    by_user = sorted_slots(jnp.where(live, tile_user_block, UB), tile_item_block)
    by_item = sorted_slots(jnp.where(live, tile_item_block, IB), tile_user_block)
    table = jnp.stack(by_user + by_item)
    f32 = jnp.float32
    vmem = pl.BlockSpec(memory_space=pltpu.VMEM)
    dma = pltpu.SemaphoreType.DMA
    return pl.pallas_call(
        kernel,
        out_shape=[
            jax.ShapeDtypeStruct((PER_Z * T, T), f32),
            jax.ShapeDtypeStruct((T, T), f32),
        ],
        in_specs=[pl.BlockSpec(memory_space=pltpu.SMEM)] + [vmem] * 4 + [pl.BlockSpec(memory_space=pl.ANY)],
        out_specs=[vmem, vmem],
        scratch_shapes=[
            pltpu.VMEM((SLOTS, T, T), f32),
            pltpu.VMEM((SLOTS + 1, T, T), f32),
            pltpu.VMEM((LAYERS, NZ, PER_Z * T, T), f32),
            pltpu.VMEM((LAYERS, AU, T, T), f32),
            pltpu.VMEM((UB, T, 2 * T), jnp.bfloat16),
            pltpu.VMEM((IB, T, 2 * T), jnp.bfloat16),
            pltpu.VMEM((LAYERS, UB, T, T), f32),
            pltpu.VMEM((LAYERS, IB, T, T), f32),
            pltpu.VMEM((LAYERS, 2, NZ - 1, RC, ROWS, T), f32),
            pltpu.VMEM((LAYERS, CHIPS, T, T), f32),
            pltpu.VMEM((LAYERS, CHIPS - 1, T, T), f32),
            pltpu.VMEM((PER_Z * T, T), f32),
            pltpu.VMEM((T, T), f32),
            dma,
            dma((LAYERS, 4, len(AG_RIGHT))),
            dma((LAYERS, 4, (NZ - 1) * RC)),
            dma((LAYERS, 4, CHIPS)),
            dma((LAYERS, 4, CHIPS)),
        ],
        compiler_params=pltpu.CompilerParams(
            collective_id=0, has_side_effects=True, vmem_limit_bytes=62 << 20
        ),
    )(
        table, user_emb, item_emb, user_degree.reshape(PER_Z, T), item_degree.reshape(1, T), tiles
    )


def solution(mesh):
    in_specs = (
        P(("au", "ia"), None),
        P(("ia", "au"), None),
        P(("au", "ia")),
        P(("ia", "au")),
        P(("au", "ia"), None, None),
        P(("au", "ia")),
        P(("au", "ia")),
        P(("au", "ia")),
    )
    out_specs = (P(("au", "ia"), None), P(("ia", "au"), None))
    return jax.shard_map(
        per_device, mesh=mesh, in_specs=in_specs, out_specs=out_specs, check_vma=False
    )
```

```python
import functools
import heapq

import jax
import jax.numpy as jnp
from jax import lax
from jax.experimental import pallas as pl
from jax.experimental.pallas import tpu as pltpu
from jax.sharding import PartitionSpec as P

MESH = pl.DeviceIdType.MESH
LAYERS = 2
T = 128
NZ = 8
NX, NY = 4, 4
CHIPS = NX * NY
AU = 2 * CHIPS
UB = 32
IB = 32
SLOTS = 128
PER_Z = UB // NZ
RC = 4
ROWS = PER_Z * T // (2 * RC)
OFFSETS = sorted(
    ((dx, dy) for dx in range(NX) for dy in range(NY)),
    key=lambda o: -(min(o[0], NX - o[0]) + min(o[1], NY - o[1])),
)
PEERS = OFFSETS[:-1]
AG_RIGHT = [(s, c) for s in range(NZ // 2) for c in range(PER_Z) if s < NZ // 2 - 1 or c < PER_Z // 2]
AG_LEFT = [(s, c) for s in range(NZ // 2) for c in range(PER_Z) if s < NZ // 2 - 1 or c >= PER_Z // 2]
PIECE = 32
UNROLL = 32


def halves(value):
    high = value.astype(jnp.bfloat16)
    low = (value - high.astype(jnp.float32)).astype(jnp.bfloat16)
    return jnp.concatenate([high, low], axis=1)


def column(row):
    return jnp.transpose(jnp.broadcast_to(row, (T, T)))


def merge(chains):
    heap = []
    for at, (start, gen) in enumerate(chains):
        heap.append((start, at, gen))
    heapq.heapify(heap)
    while heap:
        when, at, gen = heapq.heappop(heap)
        step = next(gen, None)
        if step is not None:
            heapq.heappush(heap, (when + step, at, gen))


class Place:
    def __init__(self):
        self.au = lax.axis_index("au")
        self.z = lax.axis_index("ia")
        self.core = lax.rem(self.au, 2)
        self.x = lax.rem(self.au // 2, NX)
        self.y = self.au // (2 * NX)
        self.partner = self.au + 1 - 2 * self.core

    def chip(self, dx, dy):
        return lax.rem(self.y + dy, NY) * NX + lax.rem(self.x + dx, NX)

    def ring(self, step):
        return lax.rem(self.z + NZ + step, NZ)


class GatherZ:
    def __init__(self, me, buf, sems, on_chunk):
        self.me, self.buf, self.sems, self.on_chunk = me, buf, sems, on_chunk
        self.plans = (AG_RIGHT, AG_LEFT)

    def copy(self, way, k, received=False):
        me = self.me
        s, c = self.plans[way][k]
        sign = 1 if way == 0 else -1
        block = me.ring(-sign * (s + (1 if received else 0)))
        ref = self.buf.at[block, pl.ds(c * T, T)]
        return (
            pltpu.make_async_remote_copy(
                src_ref=ref,
                dst_ref=ref,
                send_sem=self.sems.at[2 * way, k],
                recv_sem=self.sems.at[2 * way + 1, k],
                device_id=(me.au, me.ring(sign)),
                device_id_type=MESH,
            ),
            block,
            c,
        )

    def start_own(self, c):
        for way in range(2):
            self.copy(way, self.plans[way].index((0, c)))[0].start()

    def run(self, dt):
        order = []
        for k in range(len(AG_RIGHT)):
            order += [(0, k), (1, k)]
        for way, k in order:
            yield dt / 2
            s, c = self.plans[way][k]
            copy, block, c = self.copy(way, k, received=True)
            copy.wait_recv()
            if (s + 1, c) in self.plans[way]:
                self.copy(way, self.plans[way].index((s + 1, c)))[0].start()
            self.on_chunk(block, c)

    def finish(self):
        for way in range(2):
            for k in range(len(self.plans[way])):
                self.copy(way, k)[0].wait_send()


class ScatterZ:
    def __init__(self, me, q, land, sems, on_final):
        self.me, self.q, self.land, self.sems, self.on_final = me, q, land, sems, on_final

    def part(self, block, way, c):
        rows = way * RC * ROWS + c * ROWS
        return self.q.at[block * PER_Z + rows // T, pl.ds(rows % T, ROWS)]

    def copy(self, way, s, c):
        me = self.me
        sign = 1 if way == 0 else -1
        if s == 0:
            src = self.part(me.ring(-sign), way, c)
        else:
            src = self.land.at[way, s - 1, c]
        return pltpu.make_async_remote_copy(
            src_ref=src,
            dst_ref=self.land.at[way, s, c],
            send_sem=self.sems.at[2 * way, s * RC + c],
            recv_sem=self.sems.at[2 * way + 1, s * RC + c],
            device_id=(me.au, me.ring(sign)),
            device_id_type=MESH,
        )

    def start(self):
        for c in range(RC):
            for way in range(2):
                self.copy(way, 0, c).start()

    def run(self, dt):
        me = self.me
        for s in range(NZ - 1):
            for c in range(RC):
                for way in range(2):
                    yield dt / 2
                    sign = 1 if way == 0 else -1
                    self.copy(way, s, c).wait_recv()
                    mine = self.part(me.ring(-sign * (s + 2)), way, c)
                    value = self.land[way, s, c] + mine[...]
                    if s < NZ - 2:
                        self.land[way, s, c] = value
                        self.copy(way, s + 1, c).start()
                    else:
                        self.on_final(way * RC * ROWS + c * ROWS, value)

    def finish(self):
        for s in range(NZ - 1):
            for c in range(RC):
                for way in range(2):
                    self.copy(way, s, c).wait_send()


class GatherPlane:
    def __init__(self, me, buf, sems, on_block):
        self.me, self.buf, self.sems, self.on_block = me, buf, sems, on_block

    def send(self, k):
        me = self.me
        dx, dy = PEERS[k]
        ref = self.buf.at[me.au]
        return pltpu.make_async_remote_copy(
            src_ref=ref, dst_ref=ref,
            send_sem=self.sems.at[0, k], recv_sem=self.sems.at[1, k],
            device_id=(2 * me.chip(dx, dy) + me.core, me.z), device_id_type=MESH,
        )

    def source(self, k):
        dx, dy = OFFSETS[k]
        return 2 * self.me.chip(NX - dx, NY - dy)

    def landed(self, k):
        me = self.me
        dx, dy = PEERS[k]
        ref = self.buf.at[self.source(k) + me.core]
        return pltpu.make_async_remote_copy(
            src_ref=ref, dst_ref=ref,
            send_sem=self.sems.at[0, k], recv_sem=self.sems.at[1, k],
            device_id=(2 * me.chip(dx, dy) + me.core, me.z), device_id_type=MESH,
        )

    def across(self, k, received=False):
        me = self.me
        side = 1 - me.core if received else me.core
        ref = self.buf.at[self.source(k) + side]
        return pltpu.make_async_remote_copy(
            src_ref=ref, dst_ref=ref,
            send_sem=self.sems.at[2, k], recv_sem=self.sems.at[3, k],
            device_id=(me.partner, me.z), device_id_type=MESH,
        )

    def start(self):
        for k in range(len(PEERS)):
            self.send(k).start()
        self.across(CHIPS - 1).start()

    def run(self, dt, dt_across):
        me = self.me
        self.on_block(me.au)
        yield 2.0
        for k in range(len(PEERS)):
            yield dt
            self.landed(k).wait_recv()
            self.across(k).start()
            self.on_block(self.source(k) + me.core)
        for k in [CHIPS - 1] + list(range(len(PEERS))):
            yield dt_across
            self.across(k, received=True).wait_recv()
            self.on_block(self.source(k) + 1 - me.core)

    def finish(self):
        for k in range(len(PEERS)):
            self.send(k).wait_send()
        for k in range(CHIPS):
            self.across(k).wait_send()


class ScatterPlane:
    def __init__(self, me, p, pair, home, sems, on_final):
        self.me, self.p, self.pair, self.home = me, p, pair, home
        self.sems, self.on_final = sems, on_final

    def across(self, k):
        me = self.me
        dx, dy = OFFSETS[k]
        return pltpu.make_async_remote_copy(
            src_ref=self.p.at[2 * me.chip(dx, dy) + 1 - me.core], dst_ref=self.pair.at[k],
            send_sem=self.sems.at[0, k], recv_sem=self.sems.at[1, k],
            device_id=(me.partner, me.z), device_id_type=MESH,
        )

    def send(self, k):
        me = self.me
        dx, dy = PEERS[k]
        return pltpu.make_async_remote_copy(
            src_ref=self.pair.at[k], dst_ref=self.home.at[k],
            send_sem=self.sems.at[2, k], recv_sem=self.sems.at[3, k],
            device_id=(2 * me.chip(dx, dy) + me.core, me.z), device_id_type=MESH,
        )

    def start(self):
        for k in range(CHIPS):
            self.across(k).start()

    def run(self, dt_across, dt):
        me = self.me
        for k in range(CHIPS):
            yield dt_across
            self.across(k).wait_recv()
            dx, dy = OFFSETS[k]
            self.pair[k] = self.pair[k] + self.p[2 * me.chip(dx, dy) + me.core]
            if k < len(PEERS):
                self.send(k).start()
        for k in range(len(PEERS)):
            yield dt
            self.send(k).wait_recv()
            self.pair[CHIPS - 1] = self.pair[CHIPS - 1] + self.home[k]
        self.on_final(self.pair[CHIPS - 1])

    def finish(self):
        for k in range(CHIPS):
            self.across(k).wait_send()
        for k in range(len(PEERS)):
            self.send(k).wait_send()


def kernel(
    table, user_emb, item_emb, user_degree, item_degree, tiles_hbm,
    user_out, item_out,
    tiles, run, ug, vg, u2, v2, q, p, land, pair, home, user_scale, item_scale,
    tile_sem, gz_sems, sz_sems, gp_sems, sp_sems,
):
    me = Place()
    load = pltpu.make_async_copy(tiles_hbm, tiles, tile_sem)
    load.start()

    barrier = pltpu.get_barrier_semaphore()
    greeted = [(me.au, me.ring(1)), (me.au, me.ring(-1)), (me.partner, me.z)]
    greeted += [(2 * me.chip(dx, dy) + me.core, me.z) for dx, dy in PEERS]
    for device in greeted:
        pl.semaphore_signal(barrier, inc=1, device_id=device, device_id_type=MESH)

    item_scale[...] = column(lax.rsqrt(item_degree[...].astype(jnp.float32)))
    vg[0, me.au] = item_emb[...] * item_scale[...]
    for c in range(PER_Z):
        rows = pl.ds(c * T, T)
        user_scale[rows] = column(lax.rsqrt(user_degree[c : c + 1].astype(jnp.float32)))
        ug[0, me.z, rows] = user_emb[rows] * user_scale[rows]
    user_out[...] = user_emb[...]
    item_out[...] = item_emb[...]
    run[0] = jnp.zeros((T, T), jnp.float32)
    pl.semaphore_wait(barrier, len(greeted))

    def user_chunk(layer):
        def take(block, c):
            u2[block * PER_Z + c] = halves(ug[layer, block, pl.ds(c * T, T)])
        return take

    def item_block(layer):
        def take(block):
            v2[block] = halves(vg[layer, block])
        return take

    gather_z = [GatherZ(me, ug.at[l], gz_sems.at[l], user_chunk(l)) for l in range(LAYERS)]
    gather_plane = [GatherPlane(me, vg.at[l], gp_sems.at[l], item_block(l)) for l in range(LAYERS)]

    def user_final(layer):
        last = layer + 1 == LAYERS
        def take(row, value):
            rows = pl.ds(row, ROWS)
            scale = user_scale[rows]
            now = value * scale
            total = user_out[rows] + now
            user_out[rows] = total * (1.0 / (LAYERS + 1.0)) if last else total
            if not last:
                ug[layer + 1, me.z, rows] = now * scale
                if (row + ROWS) % T == 0:
                    gather_z[layer + 1].start_own(row // T)
                    user_chunk(layer + 1)(me.z, row // T)
        return take

    def item_final(layer):
        last = layer + 1 == LAYERS
        def take(value):
            now = value * item_scale[...]
            total = item_out[...] + now
            item_out[...] = total * (1.0 / (LAYERS + 1.0)) if last else total
            if not last:
                vg[layer + 1, me.au] = now * item_scale[...]
                gather_plane[layer + 1].start()
        return take

    scatter_z = [ScatterZ(me, q.at[l], land.at[l], sz_sems.at[l], user_final(l)) for l in range(LAYERS)]
    scatter_plane = [
        ScatterPlane(me, p.at[l], pair.at[l], home.at[l], sp_sems.at[l], item_final(l)) for l in range(LAYERS)
    ]

    def products(kind, source, out, dt):
        base = 4 * kind
        def step(at, carry):
            acc = run[at * UNROLL]
            for i in range(UNROLL):
                slot = at * UNROLL + i
                w = tiles[table[base, slot]]
                if kind == 1:
                    w = jnp.transpose(w)
                rows = source[table[base + 1, slot]]
                wide = jnp.dot(
                    halves(w), jnp.concatenate([rows, rows], axis=0), preferred_element_type=jnp.float32
                )
                keep = table[base + 2, slot].astype(jnp.float32)
                acc = acc * keep + (wide[:, :T] + wide[:, T:])
                run[slot + 1] = acc
            return carry
        per = PIECE // UNROLL
        for piece in range(SLOTS // PIECE):
            yield dt
            lax.fori_loop(piece * per, (piece + 1) * per, step, 0)
        def pick(block, carry):
            out[block] = run[table[base + 3, block]]
            return carry
        yield 0.4
        lax.fori_loop(0, UB, pick, 0)

    for c in range(PER_Z):
        gather_z[0].start_own(c)
        user_chunk(0)(me.z, c)
    gather_plane[0].start()

    def items_then_products(layer, first):
        yield 1e-3
        yield from first
        yield from gather_plane[layer].run(0.9, 0.1)
        if layer == 0:
            load.wait()
        yield from products(0, v2, q.at[layer], 0.9)
        scatter_z[layer].start()

    def empty():
        return
        yield

    merge([(0.0, items_then_products(0, empty())), (1.0, gather_z[0].run(1.45))])

    def plane_chain():
        yield from products(1, u2, p.at[0], 0.9)
        scatter_plane[0].start()
        yield from items_then_products(1, scatter_plane[0].run(0.3, 0.7))

    def z_chain():
        yield from scatter_z[0].run(0.72)
        yield from gather_z[1].run(1.45)

    merge([(0.0, plane_chain()), (1.0, z_chain())])

    def last_plane():
        yield from products(1, u2, p.at[1], 0.9)
        scatter_plane[1].start()
        yield from scatter_plane[1].run(0.3, 0.7)

    merge([(0.0, last_plane()), (1.0, scatter_z[1].run(0.72))])

    for layer in range(LAYERS):
        for chain in (gather_z, gather_plane, scatter_z, scatter_plane):
            chain[layer].finish()


def sorted_slots(keys, others):
    slots = jnp.arange(SLOTS, dtype=jnp.int32)
    before = (keys[:, None] < keys[None, :]) | (
        (keys[:, None] == keys[None, :]) & (slots[:, None] < slots[None, :])
    )
    place = jnp.sum(before.astype(jnp.int32), axis=0)
    hit = (place[:, None] == slots[None, :]).astype(jnp.int32)
    order = jnp.sum(hit * slots[:, None], axis=0)
    block = jnp.sum(hit * others[:, None], axis=0)
    key_sorted = jnp.sum(hit * keys[:, None], axis=0)
    first = jnp.sum((keys[:, None] < key_sorted[None, :]).astype(jnp.int32), axis=0) == slots
    upto = jnp.sum((keys[:, None] <= slots[None, :]).astype(jnp.int32), axis=0)
    any_of = jnp.sum((keys[:, None] == slots[None, :]).astype(jnp.int32), axis=0) > 0
    return [order, block, 1 - first.astype(jnp.int32), jnp.where(any_of, upto, 0)]


def per_device(
    user_emb, item_emb, user_degree, item_degree, tiles, tile_user_block, tile_item_block, live_tiles
):
    live = jnp.arange(SLOTS, dtype=jnp.int32) < live_tiles[0]
    by_user = sorted_slots(jnp.where(live, tile_user_block, UB), tile_item_block)
    by_item = sorted_slots(jnp.where(live, tile_item_block, IB), tile_user_block)
    table = jnp.stack(by_user + by_item)
    f32 = jnp.float32
    vmem = pl.BlockSpec(memory_space=pltpu.VMEM)
    dma = pltpu.SemaphoreType.DMA
    return pl.pallas_call(
        kernel,
        out_shape=[
            jax.ShapeDtypeStruct((PER_Z * T, T), f32),
            jax.ShapeDtypeStruct((T, T), f32),
        ],
        in_specs=[pl.BlockSpec(memory_space=pltpu.SMEM)] + [vmem] * 4 + [pl.BlockSpec(memory_space=pl.ANY)],
        out_specs=[vmem, vmem],
        scratch_shapes=[
            pltpu.VMEM((SLOTS, T, T), f32),
            pltpu.VMEM((SLOTS + 1, T, T), f32),
            pltpu.VMEM((LAYERS, NZ, PER_Z * T, T), f32),
            pltpu.VMEM((LAYERS, AU, T, T), f32),
            pltpu.VMEM((UB, T, 2 * T), jnp.bfloat16),
            pltpu.VMEM((IB, T, 2 * T), jnp.bfloat16),
            pltpu.VMEM((LAYERS, UB, T, T), f32),
            pltpu.VMEM((LAYERS, IB, T, T), f32),
            pltpu.VMEM((LAYERS, 2, NZ - 1, RC, ROWS, T), f32),
            pltpu.VMEM((LAYERS, CHIPS, T, T), f32),
            pltpu.VMEM((LAYERS, CHIPS - 1, T, T), f32),
            pltpu.VMEM((PER_Z * T, T), f32),
            pltpu.VMEM((T, T), f32),
            dma,
            dma((LAYERS, 4, len(AG_RIGHT))),
            dma((LAYERS, 4, (NZ - 1) * RC)),
            dma((LAYERS, 4, CHIPS)),
            dma((LAYERS, 4, CHIPS)),
        ],
        compiler_params=pltpu.CompilerParams(
            collective_id=0, has_side_effects=True, vmem_limit_bytes=62 << 20
        ),
    )(
        table, user_emb, item_emb, user_degree.reshape(PER_Z, T), item_degree.reshape(1, T), tiles
    )


def solution(mesh):
    in_specs = (
        P(("au", "ia"), None),
        P(("ia", "au"), None),
        P(("au", "ia")),
        P(("ia", "au")),
        P(("au", "ia"), None, None),
        P(("au", "ia")),
        P(("au", "ia")),
        P(("au", "ia")),
    )
    out_specs = (P(("au", "ia"), None), P(("ia", "au"), None))
    return jax.shard_map(
        per_device, mesh=mesh, in_specs=in_specs, out_specs=out_specs, check_vma=False
    )
```
